32 devices in a mesh: row: 4 (over z), col: 8 (over y, x, core).
Axes of the slice: x: 2, y: 2, z: 4, core: 2. Of those that a mesh axis runs over, the one named last changes fastest.
Arguments:
- src_feats: bfloat16 [65536, 128], P(('row', 'col')), may hold values from -32 to 32
- dst_feats: bfloat16 [2048, 128], P(('row', 'col')), may hold values from -6 to 6
- proj_weight: bfloat16 [128, 256], replicated, may hold values from -0.5 to 0.5
- attn_src: float32 [4, 64], replicated, may hold values from -1.5 to 1.5
- attn_dst: float32 [4, 64], replicated, may hold values from -2 to 2
- tile_dst: int32 [4, 2048], P('row', 'col'), may hold values from 0 to 3, as said below
- tile_src: int32 [4, 2048], P('row', 'col'), may hold values from 0 to 63
- tile_live: int32 [4, 8], P('row', 'col'), may hold values from 64 to 256, as said below
- tile_mask: int32 [4, 2048, 2048], P('row', 'col'), may hold values from 0 to 255, as said below
Outputs:
- attended: bfloat16 [2048, 256], P(('row', 'col'))
The draws below stay inside these ranges and needn't reach their ends.
Inputs may be any that keep to these rules, and one draw needn't show every extreme that they name: The pairs (tile_dst, tile_src) of one device's 256 slots are distinct. `tile_live`: in every draw some device has all 256 slots live. `tile_mask`: each word holds the edge bits of 8 consecutive source columns of one destination row of a tile in its lowest 8 bits; slots at or past a device's live count carry arbitrary bits.
All inputs are finite; a program needn't handle non-finite values.
Results may differ from the reference program's by a relative error of at most 0.015.
Values may be sent and summed in bfloat16 or wider, within the bound.
A program may use at most 64 MiB of HBM per device.

```python
import math
import jax
import jax.numpy as jnp
from jax import lax

F_IN = 128
HEADS = 4
HEAD_DIM = 64
DST_DEV = 512
SRC_COL = 8192
TILES = 256
NDST = 2048
N_ROW = 4
N_COL = 8


def base_params(draw_key):
    weight_key = jax.random.fold_in(draw_key, 11)
    attn_key = jax.random.fold_in(draw_key, 12)
    weight = jnp.clip(jax.random.normal(weight_key, (F_IN, HEADS * HEAD_DIM), jnp.float32) / math.sqrt(F_IN), -0.5, 0.5)
    attention = jnp.clip(0.35 * jax.random.normal(attn_key, (HEADS, HEAD_DIM), jnp.float32), -1.5, 1.5)
    return (weight, attention)


def draw_proj_weight(draw_key, part_index):
    weight, attention = base_params(draw_key)
    return weight.astype(jnp.bfloat16)


def draw_attn_src(draw_key, part_index):
    weight, attention = base_params(draw_key)
    return attention


def draw_src_feats(draw_key, part_index):
    row_total = SRC_COL * N_COL
    sign_bits = jax.random.randint(jax.random.fold_in(draw_key, 44), (F_IN,), 0, 2, dtype=jnp.int32)
    signs = jnp.where(sign_bits == 0, -1.0, 1.0).astype(jnp.float32)
    offset = signs * jax.random.uniform(jax.random.fold_in(draw_key, 45), (F_IN,), jnp.float32, 1.0, 2.0)
    noise_rows = jnp.clip(jax.random.normal(jax.random.fold_in(draw_key, 43), (row_total, F_IN), jnp.float32), -6.0, 6.0)
    feats = offset[None, :] + 0.5 * noise_rows
    return jnp.clip(feats, -32.0, 32.0).astype(jnp.bfloat16)


def tile_layout(draw_key):
    blocks = DST_DEV // 128
    src_blocks = SRC_COL // 128
    device_keys = jax.random.split(jax.random.fold_in(draw_key, 21), N_ROW * N_COL)
    orders = jax.vmap(lambda device_key: jax.random.permutation(device_key, blocks * src_blocks)[:TILES])(device_keys)
    orders = orders.reshape(N_ROW, N_COL * TILES).astype(jnp.int32)
    return (orders // src_blocks, orders % src_blocks)


def draw_tile_dst(draw_key, part_index):
    return tile_layout(draw_key)[0]


def draw_tile_src(draw_key, part_index):
    return tile_layout(draw_key)[1]


def live_counts(draw_key):
    lowest = max(1, TILES // 4)
    jitter_top = max(1, TILES // 8)
    bases = jax.random.randint(jax.random.fold_in(draw_key, 31), (N_ROW,), lowest, TILES // 2 + 1, dtype=jnp.int32)
    jitters = jax.random.randint(jax.random.fold_in(draw_key, 33), (N_ROW, N_COL), 0, jitter_top, dtype=jnp.int32)
    counts = bases[:, None] + jitters
    full_row = jax.random.randint(jax.random.fold_in(draw_key, 32), (), 0, N_ROW, dtype=jnp.int32)
    low_column = jax.random.randint(jax.random.fold_in(draw_key, 34), (), 0, N_COL, dtype=jnp.int32)
    row_iota = jnp.arange(N_ROW, dtype=jnp.int32)[:, None]
    column_iota = jnp.arange(N_COL, dtype=jnp.int32)[None, :]
    counts = jnp.where(row_iota == full_row, TILES, counts)
    low_place = (row_iota == (full_row + 1) % N_ROW) & (column_iota == low_column)
    counts = jnp.where(low_place, lowest, counts)
    return counts.astype(jnp.int32)


def draw_tile_live(draw_key, part_index):
    return live_counts(draw_key)


def draw_tile_mask(draw_key, part_index):
    mask_shape = (N_ROW, N_COL * TILES, 2048)
    pair_bits = jax.random.randint(jax.random.fold_in(draw_key, 51), mask_shape, 0, 16, dtype=jnp.int32)
    for layer in range(5):
        pair_bits = pair_bits & jax.random.randint(jax.random.fold_in(draw_key, 60 + layer), mask_shape, 0, 16, dtype=jnp.int32)
    spread = pair_bits & 1 | (pair_bits & 2) << 1 | (pair_bits & 4) << 2 | (pair_bits & 8) << 3
    live_words = spread * 3
    dead_words = jax.random.randint(jax.random.fold_in(draw_key, 52), mask_shape, 0, 256, dtype=jnp.int32)
    counts = live_counts(draw_key)
    slot_iota = jnp.arange(N_COL * TILES, dtype=jnp.int32) % TILES
    column_iota = jnp.arange(N_COL * TILES, dtype=jnp.int32) // TILES
    slot_live = slot_iota[None, :] < counts[:, column_iota]
    return jnp.where(slot_live[:, :, None], live_words, dead_words).astype(jnp.int32)


def shard_levels(key, extent, shards, low, largest):
    factor_of, own = 1.0, jax.random.fold_in(key, 6)
    for position, shards_of in shards:
        steps = jnp.exp(jax.random.uniform(jax.random.fold_in(own, position), (shards_of,), jnp.float32, low / len(shards), largest / len(shards)))
        factor_of = factor_of * jnp.repeat(steps, extent[position] // shards_of).reshape([-1 if axis == position else 1 for axis in range(len(extent))])
    return factor_of


def centred(own_key, shape, width, reach, cuts=(), held_as=jnp.bfloat16):
    gain = shard_levels(own_key, shape, cuts, -0.22, 0.18) if cuts else 1.0
    drawn = jax.random.normal(own_key, shape, jnp.float32) * width * gain
    return jnp.minimum(jnp.maximum(drawn, -reach), reach).astype(held_as)


def setup_inputs(seed: int = 0) -> dict:
    arg_keys = jax.random.split(jax.random.key(seed), 10)
    src_feats = draw_src_feats(jax.random.fold_in(arg_keys[9], 71), 0)
    dst_feats = centred(arg_keys[1], (NDST, F_IN), 1.0, 6.0, ((0, 32),))
    proj_weight = draw_proj_weight(jax.random.fold_in(arg_keys[9], 71), 0)
    attn_src = draw_attn_src(jax.random.fold_in(arg_keys[9], 71), 0)
    attn_dst = centred(arg_keys[4], (HEADS, HEAD_DIM), 0.35, 2.0, (), jnp.float32)
    tile_dst = draw_tile_dst(jax.random.fold_in(arg_keys[9], 71), 0)
    tile_src = draw_tile_src(jax.random.fold_in(arg_keys[9], 71), 0)
    tile_live = draw_tile_live(jax.random.fold_in(arg_keys[9], 71), 0)
    tile_mask = draw_tile_mask(jax.random.fold_in(arg_keys[9], 71), 0)
    return dict(src_feats=src_feats, dst_feats=dst_feats, proj_weight=proj_weight, attn_src=attn_src, attn_dst=attn_dst, tile_dst=tile_dst, tile_src=tile_src, tile_live=tile_live, tile_mask=tile_mask)


neg_fill = -1e30


def leaky_relu(values):
    return jnp.where(values >= 0, values, 0.2 * values)


def head_scores(hidden, attention):
    row_count = hidden.shape[0]
    return jnp.sum(hidden.astype(jnp.float32).reshape(row_count, HEADS, HEAD_DIM) * attention[None], axis=2)


def unpack_bits(packed):
    leading = packed.shape[:-1]
    shifts = jnp.arange(8, dtype=jnp.int32)
    layered = (packed.reshape(leading + (128, 16, 1)) >> shifts) & 1
    return layered.reshape(leading + (128, 128)) == 1


def reference(src_feats, dst_feats, proj_weight, attn_src, attn_dst, tile_dst, tile_src, tile_live, tile_mask):
    hidden_units = HEADS * HEAD_DIM
    blocks = DST_DEV // 128
    src_blocks = SRC_COL // 128
    portion = SRC_COL // N_ROW
    src_hidden = jnp.dot(src_feats, proj_weight, preferred_element_type=jnp.float32).astype(jnp.bfloat16)
    src_score = head_scores(src_hidden, attn_src)
    dst_hidden = jnp.dot(dst_feats, proj_weight, preferred_element_type=jnp.float32).astype(jnp.bfloat16)
    dst_score = head_scores(dst_hidden, attn_dst)
    self_source = head_scores(dst_hidden, attn_src)
    slab_hidden = src_hidden.reshape(N_ROW, N_COL, portion, hidden_units).transpose(1, 0, 2, 3)
    slab_hidden = slab_hidden.reshape(N_COL, src_blocks, 128, hidden_units)
    slab_score = src_score.reshape(N_ROW, N_COL, portion, HEADS).transpose(1, 0, 2, 3)
    slab_score = slab_score.reshape(N_COL, src_blocks, 128, HEADS).transpose(0, 1, 3, 2)
    dest_table = dst_score.reshape(N_ROW, blocks, 128, HEADS).transpose(0, 1, 3, 2)
    self_table = leaky_relu(dst_score + self_source).reshape(N_ROW, blocks, 128, HEADS).transpose(0, 1, 3, 2)
    self_hidden_all = dst_hidden.reshape(N_ROW, blocks, 128, hidden_units)
    dst_slots = tile_dst.reshape(N_ROW, N_COL, TILES)
    src_slots = tile_src.reshape(N_ROW, N_COL, TILES)
    mask_slots = tile_mask.reshape(N_ROW, N_COL, TILES, 2048)
    slot_index = jnp.arange(TILES, dtype=jnp.int32)

    def tile_terms(dest_rows, column_scores, dest_ids, source_ids, live_count, packed):
        dest_part = dest_rows[dest_ids]
        source_part = column_scores[source_ids]
        scores = leaky_relu(dest_part[:, :, :, None] + source_part[:, :, None, :])
        present = unpack_bits(packed) & (slot_index < live_count)[:, None, None]
        return scores, present[:, None]

    def one_row(inputs):
        dest_rows, self_rows, self_hidden, dest_all, source_all, live_all, packed_all = inputs

        def max_step(running, column):
            column_scores, dest_ids, source_ids, live_count, packed = column
            scores, present = tile_terms(dest_rows, column_scores, dest_ids, source_ids, live_count, packed)
            tile_top = jnp.max(jnp.where(present, scores, neg_fill), axis=3)
            return running.at[dest_ids].max(tile_top), None

        initial_max = jnp.full((blocks, HEADS, 128), neg_fill, jnp.float32)
        edge_max = lax.scan(max_step, initial_max, (slab_score, dest_all, source_all, live_all, packed_all))[0]
        row_max = jnp.maximum(edge_max, self_rows)

        def sum_step(state_in, column):
            den_sum, num_sum = state_in
            column_scores, column_hidden, dest_ids, source_ids, live_count, packed = column
            scores, present = tile_terms(dest_rows, column_scores, dest_ids, source_ids, live_count, packed)
            weights = jnp.where(present, jnp.exp(scores - row_max[dest_ids][:, :, :, None]), 0.0)
            den_sum = den_sum.at[dest_ids].add(jnp.sum(weights, axis=3))
            rounded = lax.optimization_barrier(weights.astype(jnp.bfloat16)).astype(jnp.float32)
            values = column_hidden[source_ids].astype(jnp.float32).reshape(TILES, 128, HEADS, HEAD_DIM)
            products = jnp.einsum("khij,kjhd->kihd", rounded, values)
            num_sum = num_sum.at[dest_ids].add(products.reshape(TILES, 128, hidden_units))
            return (den_sum, num_sum), None

        initial_sums = (jnp.zeros((blocks, HEADS, 128), jnp.float32), jnp.zeros((blocks, 128, hidden_units), jnp.float32))
        den_sum, num_sum = lax.scan(sum_step, initial_sums, (slab_score, slab_hidden, dest_all, source_all, live_all, packed_all))[0]
        self_weight = jnp.exp(self_rows - row_max)
        den_sum = den_sum + self_weight
        rounded_self = lax.optimization_barrier(self_weight.astype(jnp.bfloat16)).astype(jnp.float32)
        num_total = num_sum.reshape(blocks, 128, HEADS, HEAD_DIM) + rounded_self.transpose(0, 2, 1)[:, :, :, None] * self_hidden.astype(jnp.float32).reshape(blocks, 128, HEADS, HEAD_DIM)
        result = num_total / den_sum.transpose(0, 2, 1)[:, :, :, None]
        return result.reshape(DST_DEV, hidden_units).astype(jnp.bfloat16)

    outputs = lax.map(one_row, (dest_table, self_table, self_hidden_all, dst_slots, src_slots, tile_live, mask_slots))
    return outputs.reshape(N_ROW * DST_DEV, hidden_units)
```

```python
import functools
import jax
import jax.numpy as jnp
from jax import lax
from jax.experimental import pallas as pl
from jax.experimental.pallas import tpu as pltpu
from jax.sharding import PartitionSpec as P

BF = jnp.bfloat16
F32 = jnp.float32
NEG = -1e30
SPAN = 40.0
GROUP = 4


def leaky(x):
    return jnp.maximum(x, 0.2 * x)


def split3(x):
    first = x.astype(BF)
    rest = x - first.astype(F32)
    second = rest.astype(BF)
    third = (rest - second.astype(F32)).astype(BF)
    return first, second, third


def dot(a, b):
    return jnp.dot(a, b, preferred_element_type=F32)


def dot_exact(a, b32):
    return sum(dot(a, part) for part in split3(b32))


def order_matrix(rows, inverse):
    per = rows // 8
    a = lax.broadcasted_iota(jnp.int32, (rows, rows), 0)
    b = lax.broadcasted_iota(jnp.int32, (rows, rows), 1)
    if inverse:
        a, b = b, a
    return jnp.where(b == (a % per) * 8 + a // per, 1.0, 0.0).astype(BF)


def main_kernel(
    heads, inv_ref, feats_ref, dst_ref, weight_ref, asrc_ref, adst_ref, expand_ref, packed_ref,
    out_ref, mask_ref, value_ref, score_ref, factor_ref, fa_ref, fc_ref, d_ref, m_ref, w_ref,
    acc_ref, sems
):
    units = weight_ref.shape[1]
    slabs = feats_ref.shape[0]
    nsb = slabs // 128
    nd = dst_ref.shape[0]
    blocks = nd // 128
    slots = packed_ref.shape[0]
    pitch = mask_ref.shape[0] // 16
    half = units // heads
    copies = [
        pltpu.make_async_copy(
            packed_ref.at[:, pl.ds(u * 128, 128)], mask_ref.at[pl.ds(u * pitch, slots), :], sems.at[u]
        )
        for u in range(16)
    ]
    for copy in copies:
        copy.start()
    for u in range(16):
        mask_ref[u * pitch + slots : (u + 1) * pitch, :] = jnp.zeros((pitch - slots, 128), jnp.int32)

    lane = lax.broadcasted_iota(jnp.int32, (1, 128), 1)
    weight = weight_ref[...]
    arows = asrc_ref[...]
    a_parts = jnp.concatenate([p.astype(F32) for p in split3(arows)] + [jnp.zeros_like(arows)], 0).astype(BF)
    chunk = 512

    def project(k, carry):
        rows = pl.ds(pl.multiple_of(k * chunk, chunk), chunk)
        hidden = dot(feats_ref[rows, :], weight).astype(BF)
        parts = lax.dot_general(
            a_parts, hidden, (((1,), (1,)), ((), ())), preferred_element_type=F32
        )
        score_ref[:, rows] = parts[0:8] + parts[8:16] + parts[16:24]
        for h in range(heads):
            tile = hidden[:, (h // 2) * 128 : (h // 2) * 128 + 128]
            own = (lane >= half) if h % 2 else (lane < half)
            value_ref[rows, h * 128 : h * 128 + 128] = jnp.where(own, tile.astype(F32), 1.0).astype(BF)
        return carry

    lax.fori_loop(0, slabs // chunk, project, 0)
    scores = score_ref[0:heads, :]
    top = jnp.max(scores, axis=1, keepdims=True)
    low = jnp.min(scores, axis=1, keepdims=True)
    wide = jnp.max(top - low) > SPAN
    near = scores - top
    factor_ref[0:heads, :] = jnp.exp(near)
    factor_ref[heads : 2 * heads, :] = jnp.exp(0.2 * near)

    perm = order_matrix(128, False)
    dst_hidden = jnp.concatenate(
        [
            dot(dot(perm, dst_ref[b * 128 : b * 128 + 128, :]).astype(BF), weight).astype(BF)
            for b in range(blocks)
        ],
        0,
    )
    d_ref[...] = dot_exact(dst_hidden, adst_ref[...])
    acc_ref[...] = jnp.zeros_like(acc_ref)
    for copy in copies:
        copy.wait()

    bit_row = jnp.left_shift(1, lax.broadcasted_iota(jnp.int32, (1, 1024), 1) % 8)

    def bits(q, bs):
        words = [mask_ref[pl.ds(inv_ref[b * nsb + q], 16, stride=pitch), :] for b in bs]
        words = jnp.concatenate(words, 0) if len(words) > 1 else words[0]
        spread = dot(words.astype(F32).astype(BF), expand_ref[...]).astype(jnp.int32)
        return jnp.where((spread & bit_row) != 0, 1.0, 0.0)

    def tile_of(flags, k):
        return jnp.concatenate([flags[16 * k : 16 * k + 16, 128 * r : 128 * r + 128] for r in range(8)], 0)

    @pl.when(jnp.logical_not(wide))
    def _():
        for h in range(heads):
            cols = slice(h * 128, h * 128 + 128)
            t = d_ref[:, cols] + top[h : h + 1, :]
            m = leaky(t)
            m_ref[:, cols] = m
            fa_ref[:, cols] = jnp.exp(t - m).astype(BF)
            fc_ref[:, cols] = jnp.exp(0.2 * t - m).astype(BF)

        def step(g, carry):
            for qq in range(GROUP):
                q = g * GROUP + qq
                flags = bits(q, range(blocks))
                tiles = [tile_of(flags, b).astype(BF).reshape(8, 16, 128) for b in range(blocks)]
                place = pl.ds(pl.multiple_of(q * 128, 128), 128)
                rows = factor_ref[:, place]
                for h in range(heads):
                    cols = slice(h * 128, h * 128 + 128)
                    fb = jnp.broadcast_to(rows[h : h + 1], (16, 128)).astype(BF)[None]
                    fd = jnp.broadcast_to(rows[heads + h : heads + h + 1], (16, 128)).astype(BF)[None]
                    for b in range(blocks):
                        rs = slice(b * 128, b * 128 + 128)
                        fa = fa_ref[rs, cols].reshape(8, 16, 128)
                        fc = fc_ref[rs, cols].reshape(8, 16, 128)
                        w = jnp.maximum(fa * fb, fc * fd) * tiles[b]
                        w_ref[h, rs, qq * 128 : qq * 128 + 128] = w.reshape(128, 128)
            span = pl.ds(pl.multiple_of(g * GROUP * 128, GROUP * 128), GROUP * 128)
            for h in range(heads):
                cols = slice(h * 128, h * 128 + 128)
                acc_ref[:, cols] += dot(w_ref[h], value_ref[span, cols])
            return carry

        lax.fori_loop(0, nsb // GROUP, step, 0)

    @pl.when(wide)
    def _():
        for b in range(blocks):
            rs = slice(b * 128, b * 128 + 128)
            for h in range(heads):
                cols = slice(h * 128, h * 128 + 128)

                def top_step(q, best):
                    flag = tile_of(bits(q, (b,)), 0) > 0.5
                    s = score_ref[h : h + 1, pl.ds(pl.multiple_of(q * 128, 128), 128)]
                    return jnp.maximum(best, jnp.where(flag, s, NEG))

                best = lax.fori_loop(0, nsb, top_step, jnp.full((128, 128), NEG, F32))
                d = d_ref[rs, cols]
                m = leaky(d + jnp.max(best, axis=1, keepdims=True))
                m_ref[rs, cols] = m

                def sum_step(q, total):
                    flag = tile_of(bits(q, (b,)), 0) > 0.5
                    place = pl.ds(pl.multiple_of(q * 128, 128), 128)
                    s = score_ref[h : h + 1, place]
                    w = jnp.where(flag, jnp.exp(leaky(d + s) - m), 0.0).astype(BF)
                    return total + dot(w, value_ref[place, cols])

                acc_ref[rs, cols] = lax.fori_loop(0, nsb, sum_step, jnp.zeros((128, 128), F32))

    back = order_matrix(128, True)
    for b in range(blocks):
        rs = slice(b * 128, b * 128 + 128)
        nums = []
        aux = jnp.zeros((128, 128), F32)
        for h in range(heads):
            cols = slice(h * 128, h * 128 + 128)
            acc = acc_ref[rs, cols]
            nums.append(acc)
            first, second, _ = (p.astype(F32) for p in split3(acc))
            base = 0 if h % 2 else half
            aux = jnp.where(lane == base + h, first, aux)
            aux = jnp.where(lane == base + 8 + h, second, aux)
            for k, part in enumerate(split3(m_ref[rs, cols])):
                aux = jnp.where(lane == 16 + 4 * k + h, part.astype(F32), aux)
        pairs = [jnp.where(lane < half, nums[2 * k], nums[2 * k + 1]) for k in range(heads // 2)]
        send = jnp.concatenate(pairs + [aux], 1).astype(BF)
        out_ref[rs, :] = dot(back, send).astype(BF)


def final_kernel(heads, peers, recv_ref, dst_ref, weight_ref, gsrc_ref, gdst_ref, out_ref):
    units = weight_ref.shape[1]
    half = units // heads
    own = dst_ref.shape[0]
    hidden = dot(dst_ref[...], weight_ref[...]).astype(BF)
    self_score = leaky(dot_exact(hidden, gdst_ref[...]) + dot_exact(hidden, gsrc_ref[...]))
    l = lax.broadcasted_iota(jnp.int32, (128, units), 0)
    h = lax.broadcasted_iota(jnp.int32, (128, units), 1) // half
    base = jnp.where(h % 2 == 1, 0, half)
    take_den = jnp.where((l == base + h) | (l == base + 8 + h), 1.0, 0.0).astype(BF)
    take_top = jnp.where((l == 16 + h) | (l == 20 + h) | (l == 24 + h), 1.0, 0.0).astype(BF)
    aux = recv_ref[:, units : units + 128]
    dens = dot(aux, take_den)
    tops = jnp.where(dens > 0, dot(aux, take_top), NEG)
    best = self_score
    for k in range(peers):
        best = jnp.maximum(best, tops[k * own : (k + 1) * own])
    self_weight = jnp.exp(self_score - best)
    den = self_weight
    num = self_weight.astype(BF).astype(F32) * hidden.astype(F32)
    for k in range(peers):
        rows = slice(k * own, (k + 1) * own)
        scale = jnp.exp(tops[rows] - best)
        den = den + dens[rows] * scale
        num = num + recv_ref[rows, 0:units].astype(F32) * scale
    out_ref[...] = (num / den).astype(BF)


def body(
    src_feats, dst_feats, proj_weight, attn_src, attn_dst, tile_dst, tile_src, tile_live, tile_mask
):
    heads, half = attn_src.shape
    units = heads * half
    peers = lax.axis_size("col")
    own = dst_feats.shape[0]
    nd = own * peers
    blocks = nd // 128
    slab = lax.all_gather(src_feats, "row", axis=0, tiled=True)
    dst_all = lax.all_gather(dst_feats, "col", axis=0, tiled=True)
    nsb = slab.shape[0] // 128
    slots = tile_mask.shape[1]
    pitch = slots + 8
    slot = jnp.arange(slots, dtype=jnp.int32)
    pair = jnp.where(slot < tile_live[0, 0], tile_dst[0] * nsb + tile_src[0], -1)
    hit = pair[None, :] == jnp.arange(blocks * nsb, dtype=jnp.int32)[:, None]
    inv = jnp.min(jnp.where(hit, slot[None, :], slots), axis=1)
    flat_src = attn_src.reshape(units)
    flat_dst = attn_dst.reshape(units)
    unit_head = jnp.arange(units) // half
    arows = jnp.where(jnp.arange(8)[:, None] == unit_head[None, :], flat_src[None, :], 0.0)
    acols = jnp.where(
        unit_head[:, None] == jnp.arange(heads * 128)[None, :] // 128, flat_dst[:, None], 0.0
    )
    same = unit_head[:, None] == unit_head[None, :]
    gsrc = jnp.where(same, flat_src[:, None], 0.0)
    gdst = jnp.where(same, flat_dst[:, None], 0.0)
    wide = jnp.arange(1024)
    expand = (
        jnp.arange(128)[:, None] == ((wide // 128) * 16 + (wide % 128) // 8)[None, :]
    ).astype(BF)
    vm = pl.BlockSpec(memory_space=pltpu.VMEM)
    send = pl.pallas_call(
        functools.partial(main_kernel, heads),
        out_shape=jax.ShapeDtypeStruct((nd, units + 128), BF),
        in_specs=[pl.BlockSpec(memory_space=pltpu.SMEM)] + [vm] * 6 + [pl.BlockSpec(memory_space=pl.ANY)],
        out_specs=vm,
        scratch_shapes=[
            pltpu.VMEM((16 * pitch, 128), jnp.int32),
            pltpu.VMEM((slab.shape[0], heads * 128), BF),
            pltpu.VMEM((8, slab.shape[0]), F32),
            pltpu.VMEM((8, slab.shape[0]), F32),
            pltpu.VMEM((nd, heads * 128), BF),
            pltpu.VMEM((nd, heads * 128), BF),
            pltpu.VMEM((nd, heads * 128), F32),
            pltpu.VMEM((nd, heads * 128), F32),
            pltpu.VMEM((heads, nd, GROUP * 128), BF),
            pltpu.VMEM((nd, heads * 128), F32),
            pltpu.SemaphoreType.DMA((16,)),
        ],
        compiler_params=pltpu.CompilerParams(vmem_limit_bytes=56 * 1024 * 1024),
    )(inv, slab, dst_all, proj_weight, arows, acols, expand, tile_mask[0])
    recv = lax.all_to_all(send, "col", split_axis=0, concat_axis=0, tiled=True)
    return pl.pallas_call(
        functools.partial(final_kernel, heads, peers),
        out_shape=jax.ShapeDtypeStruct((own, units), BF),
        in_specs=[vm] * 5,
        out_specs=vm,
    )(recv, dst_feats, proj_weight, gsrc, gdst)


def solution(mesh):
    placed = (
        P(("row", "col"), None),
        P(("row", "col"), None),
        P(),
        P(),
        P(),
        P("row", "col"),
        P("row", "col"),
        P("row", "col"),
        P("row", "col", None),
    )
    return jax.shard_map(
        body, mesh=mesh, in_specs=placed, out_specs=P(("row", "col"), None), check_vma=False
    )
```

```python
import functools
import jax
import jax.numpy as jnp
from jax import lax
from jax.experimental import pallas as pl
from jax.experimental.pallas import tpu as pltpu
from jax.sharding import PartitionSpec as P

BF = jnp.bfloat16
F32 = jnp.float32
NEG = -1e30
SPAN = 40.0
GROUP = 4


def leaky(x):
    return jnp.maximum(x, 0.2 * x)


def split3(x):
    first = x.astype(BF)
    rest = x - first.astype(F32)
    second = rest.astype(BF)
    third = (rest - second.astype(F32)).astype(BF)
    return first, second, third


def dot(a, b):
    return jnp.dot(a, b, preferred_element_type=F32)


def dot_exact(a, b32):
    return sum(dot(a, part) for part in split3(b32))


def order_matrix(rows, inverse):
    per = rows // 8
    a = lax.broadcasted_iota(jnp.int32, (rows, rows), 0)
    b = lax.broadcasted_iota(jnp.int32, (rows, rows), 1)
    if inverse:
        a, b = b, a
    return jnp.where(b == (a % per) * 8 + a // per, 1.0, 0.0).astype(BF)


def main_kernel(
    heads, inv_ref, feats_ref, dst_ref, weight_ref, asrc_ref, adst_ref, expand_ref, packed_ref,
    out_ref, mask_ref, value_ref, score_ref, d_ref, m_ref, acc_ref, sems
):
    units = weight_ref.shape[1]
    slabs = feats_ref.shape[0]
    nsb = slabs // 128
    nd = dst_ref.shape[0]
    blocks = nd // 128
    slots = packed_ref.shape[0]
    pitch = mask_ref.shape[0] // 16
    half = units // heads
    copies = [
        pltpu.make_async_copy(
            packed_ref.at[:, pl.ds(u * 128, 128)], mask_ref.at[pl.ds(u * pitch, slots), :], sems.at[u]
        )
        for u in range(16)
    ]
    for copy in copies:
        copy.start()
    for u in range(16):
        mask_ref[u * pitch + slots : (u + 1) * pitch, :] = jnp.zeros((pitch - slots, 128), jnp.int32)

    lane = lax.broadcasted_iota(jnp.int32, (1, 128), 1)
    weight = weight_ref[...]
    arows = asrc_ref[...]
    a_parts = jnp.concatenate([p.astype(F32) for p in split3(arows)] + [jnp.zeros_like(arows)], 0).astype(BF)
    chunk = 512

    def project(k, carry):
        rows = pl.ds(pl.multiple_of(k * chunk, chunk), chunk)
        hidden = dot(feats_ref[rows, :], weight).astype(BF)
        parts = lax.dot_general(
            a_parts, hidden, (((1,), (1,)), ((), ())), preferred_element_type=F32
        )
        score_ref[:, rows] = parts[0:8] + parts[8:16] + parts[16:24]
        for h in range(heads):
            tile = hidden[:, (h // 2) * 128 : (h // 2) * 128 + 128]
            own = (lane >= half) if h % 2 else (lane < half)
            value_ref[rows, h * 128 : h * 128 + 128] = jnp.where(own, tile.astype(F32), 1.0).astype(BF)
        return carry

    lax.fori_loop(0, slabs // chunk, project, 0)
    perm = order_matrix(128, False)
    dst_hidden = jnp.concatenate(
        [
            dot(dot(perm, dst_ref[b * 128 : b * 128 + 128, :]).astype(BF), weight).astype(BF)
            for b in range(blocks)
        ],
        0,
    )
    d_ref[...] = dot_exact(dst_hidden, adst_ref[...])
    acc_ref[...] = jnp.zeros_like(acc_ref)
    for copy in copies:
        copy.wait()

    bit_row = jnp.left_shift(1, lax.broadcasted_iota(jnp.int32, (1, 1024), 1) % 8)

    def bits(q, bs):
        words = [mask_ref[pl.ds(inv_ref[b * nsb + q], 16, stride=pitch), :] for b in bs]
        words = jnp.concatenate(words, 0) if len(words) > 1 else words[0]
        spread = dot(words.astype(F32).astype(BF), expand_ref[...]).astype(jnp.int32)
        return jnp.where((spread & bit_row) != 0, 1.0, 0.0)

    def tile_of(flags, k):
        return jnp.concatenate([flags[16 * k : 16 * k + 16, 128 * r : 128 * r + 128] for r in range(8)], 0)

    if True:
        for b in range(blocks):
            rs = slice(b * 128, b * 128 + 128)
            for h in range(heads):
                cols = slice(h * 128, h * 128 + 128)

                def top_step(q, best):
                    flag = tile_of(bits(q, (b,)), 0) > 0.5
                    s = score_ref[h : h + 1, pl.ds(pl.multiple_of(q * 128, 128), 128)]
                    return jnp.maximum(best, jnp.where(flag, s, NEG))

                best = lax.fori_loop(0, nsb, top_step, jnp.full((128, 128), NEG, F32))
                d = d_ref[rs, cols]
                m = leaky(d + jnp.max(best, axis=1, keepdims=True))
                m_ref[rs, cols] = m

                def sum_step(q, total):
                    flag = tile_of(bits(q, (b,)), 0) > 0.5
                    place = pl.ds(pl.multiple_of(q * 128, 128), 128)
                    s = score_ref[h : h + 1, place]
                    w = jnp.where(flag, jnp.exp(leaky(d + s) - m), 0.0).astype(BF)
                    return total + dot(w, value_ref[place, cols])

                acc_ref[rs, cols] = lax.fori_loop(0, nsb, sum_step, jnp.zeros((128, 128), F32))

    back = order_matrix(128, True)
    for b in range(blocks):
        rs = slice(b * 128, b * 128 + 128)
        nums = []
        aux = jnp.zeros((128, 128), F32)
        for h in range(heads):
            cols = slice(h * 128, h * 128 + 128)
            acc = acc_ref[rs, cols]
            nums.append(acc)
            first, second, _ = (p.astype(F32) for p in split3(acc))
            base = 0 if h % 2 else half
            aux = jnp.where(lane == base + h, first, aux)
            aux = jnp.where(lane == base + 8 + h, second, aux)
            for k, part in enumerate(split3(m_ref[rs, cols])):
                aux = jnp.where(lane == 16 + 4 * k + h, part.astype(F32), aux)
        pairs = [jnp.where(lane < half, nums[2 * k], nums[2 * k + 1]) for k in range(heads // 2)]
        send = jnp.concatenate(pairs + [aux], 1).astype(BF)
        out_ref[rs, :] = dot(back, send).astype(BF)


def final_kernel(heads, peers, recv_ref, dst_ref, weight_ref, gsrc_ref, gdst_ref, out_ref):
    units = weight_ref.shape[1]
    half = units // heads
    own = dst_ref.shape[0]
    hidden = dot(dst_ref[...], weight_ref[...]).astype(BF)
    self_score = leaky(dot_exact(hidden, gdst_ref[...]) + dot_exact(hidden, gsrc_ref[...]))
    l = lax.broadcasted_iota(jnp.int32, (128, units), 0)
    h = lax.broadcasted_iota(jnp.int32, (128, units), 1) // half
    base = jnp.where(h % 2 == 1, 0, half)
    take_den = jnp.where((l == base + h) | (l == base + 8 + h), 1.0, 0.0).astype(BF)
    take_top = jnp.where((l == 16 + h) | (l == 20 + h) | (l == 24 + h), 1.0, 0.0).astype(BF)
    aux = recv_ref[:, units : units + 128]
    dens = dot(aux, take_den)
    tops = jnp.where(dens > 0, dot(aux, take_top), NEG)
    best = self_score
    for k in range(peers):
        best = jnp.maximum(best, tops[k * own : (k + 1) * own])
    self_weight = jnp.exp(self_score - best)
    den = self_weight
    num = self_weight.astype(BF).astype(F32) * hidden.astype(F32)
    for k in range(peers):
        rows = slice(k * own, (k + 1) * own)
        scale = jnp.exp(tops[rows] - best)
        den = den + dens[rows] * scale
        num = num + recv_ref[rows, 0:units].astype(F32) * scale
    out_ref[...] = (num / den).astype(BF)

def fused_kernel(
    heads, rows_n, cols_n, inv_ref, feats_ref, own_dst_ref, weight_ref, asrc_ref, adst_ref,
    expand_ref, gsrc_ref, gdst_ref, packed_ref, out_ref, flag_ref, mask_ref, slab_ref, dst_ref,
    value_ref, score_ref, fa_ref, fc_ref, m_ref, w_ref, acc_ref, send_ref, recv_ref, mask_sems,
    feat_send, feat_recv, dst_send, dst_recv, part_send, part_recv
):
    z = lax.axis_index("row")
    c = lax.axis_index("col")
    units = weight_ref.shape[1]
    half = units // heads
    shard = feats_ref.shape[0]
    chunk = GROUP * 128
    chunks = shard // chunk
    nsb = rows_n * shard // 128
    own = own_dst_ref.shape[0]
    nd = own * cols_n
    blocks = nd // 128
    slots = packed_ref.shape[0]
    pitch = mask_ref.shape[0] // 16
    mesh_id = pl.DeviceIdType.MESH

    mask_copies = [
        pltpu.make_async_copy(
            packed_ref.at[:, pl.ds(u * 128, 128)],
            mask_ref.at[pl.ds(u * pitch, slots), :],
            mask_sems.at[u],
        )
        for u in range(16)
    ]
    for copy in mask_copies:
        copy.start()

    barrier = pltpu.get_barrier_semaphore()

    def greet_col(k, carry):
        pl.semaphore_signal(
            barrier, inc=1, device_id=(z, (c + k) % cols_n), device_id_type=mesh_id
        )
        return carry

    lax.fori_loop(1, cols_n, greet_col, 0)

    @pl.when(z > 0)
    def _():
        pl.semaphore_signal(barrier, inc=1, device_id=(z - 1, c), device_id_type=mesh_id)

    @pl.when(z < rows_n - 1)
    def _():
        pl.semaphore_signal(barrier, inc=1, device_id=(z + 1, c), device_id_type=mesh_id)

    beside = (z + rows_n - 1) // rows_n + (2 * rows_n - 2 - z) // rows_n
    pl.semaphore_wait(barrier, cols_n - 1 + beside)

    def feat_copy(src, o, ch, side):
        return pltpu.make_async_remote_copy(
            src_ref=src,
            dst_ref=slab_ref.at[pl.ds(pl.multiple_of(o * shard + ch * chunk, chunk), chunk), :],
            send_sem=feat_send.at[side, o * chunks + ch],
            recv_sem=feat_recv.at[o * chunks + ch],
            device_id=((z + 1 - 2 * side + rows_n) % rows_n, c),
            device_id_type=mesh_id,
        )

    def slab_chunk(o, ch):
        return slab_ref.at[pl.ds(pl.multiple_of(o * shard + ch * chunk, chunk), chunk), :]

    def dst_copy(k, who):
        return pltpu.make_async_remote_copy(
            src_ref=own_dst_ref,
            dst_ref=dst_ref.at[pl.ds(pl.multiple_of(who * own, own), own), :],
            send_sem=dst_send.at[k],
            recv_sem=dst_recv.at[k],
            device_id=(z, (c + k) % cols_n),
            device_id_type=mesh_id,
        )

    def send_dst(k, carry):
        dst_copy(k, c).start()
        return carry

    lax.fori_loop(1, cols_n, send_dst, 0)

    def send_own(ch, carry):
        src = feats_ref.at[pl.ds(pl.multiple_of(ch * chunk, chunk), chunk), :]

        @pl.when(z < rows_n - 1)
        def _():
            feat_copy(src, z, ch, 0).start()

        @pl.when(z > 0)
        def _():
            feat_copy(src, z, ch, 1).start()

        return carry

    lax.fori_loop(0, chunks, send_own, 0)
    dst_ref[pl.ds(pl.multiple_of(c * own, own), own), :] = own_dst_ref[...]
    for u in range(16):
        mask_ref[u * pitch + slots : (u + 1) * pitch, :] = jnp.zeros((pitch - slots, 128), jnp.int32)
    acc_ref[...] = jnp.zeros_like(acc_ref)

    lane = lax.broadcasted_iota(jnp.int32, (1, 128), 1)
    weight = weight_ref[...]
    arows = asrc_ref[...]
    a_parts = jnp.concatenate(
        [p.astype(F32) for p in split3(arows)] + [jnp.zeros_like(arows)], 0
    ).astype(BF)

    def project(x, rows):
        hidden = dot(x, weight).astype(BF)
        parts = lax.dot_general(
            a_parts, hidden, (((1,), (1,)), ((), ())), preferred_element_type=F32
        )
        score_ref[:, rows] = parts[0:8] + parts[8:16] + parts[16:24]
        for h in range(heads):
            tile = hidden[:, (h // 2) * 128 : (h // 2) * 128 + 128]
            mine = (lane >= half) if h % 2 else (lane < half)
            value_ref[rows, h * 128 : h * 128 + 128] = jnp.where(
                mine, tile.astype(F32), 1.0
            ).astype(BF)

    def project_own(ch, carry):
        rows = pl.ds(pl.multiple_of(z * shard + ch * chunk, chunk), chunk)
        project(feats_ref[pl.ds(pl.multiple_of(ch * chunk, chunk), chunk), :], rows)
        return carry

    lax.fori_loop(0, chunks, project_own, 0)
    own_scores = score_ref[:, pl.ds(pl.multiple_of(z * shard, shard), shard)]
    top = jnp.max(own_scores, axis=1, keepdims=True)

    def wait_dst(k, carry):
        dst_copy(k, (c + cols_n - k) % cols_n).wait_recv()
        return carry

    lax.fori_loop(1, cols_n, wait_dst, 0)
    perm = order_matrix(128, False)
    dst_hidden = jnp.concatenate(
        [
            dot(dot(perm, dst_ref[b * 128 : b * 128 + 128, :]).astype(BF), weight).astype(BF)
            for b in range(blocks)
        ],
        0,
    )
    d_all = dot_exact(dst_hidden, adst_ref[...])
    for h in range(heads):
        cols = slice(h * 128, h * 128 + 128)
        t = d_all[:, cols] + top[h : h + 1, :]
        m = leaky(t)
        m_ref[:, cols] = m
        fa_ref[:, cols] = jnp.exp(t - m).astype(BF)
        fc_ref[:, cols] = jnp.exp(0.2 * t - m).astype(BF)
    for copy in mask_copies:
        copy.wait()
    bit_row = jnp.left_shift(1, lax.broadcasted_iota(jnp.int32, (1, 1024), 1) % 8)

    def step(g):
        span = pl.ds(pl.multiple_of(g * chunk, chunk), chunk)
        near = score_ref[0:8, span] - top
        near_b = jnp.exp(near)
        near_d = jnp.exp(0.2 * near)
        for qq in range(GROUP):
            q = g * GROUP + qq
            words = jnp.concatenate(
                [mask_ref[pl.ds(inv_ref[b * nsb + q], 16, stride=pitch), :] for b in range(blocks)], 0
            )
            spread = dot(words.astype(F32).astype(BF), expand_ref[...]).astype(jnp.int32)
            flags = jnp.where((spread & bit_row) != 0, 1.0, 0.0)
            tiles = [
                jnp.concatenate(
                    [flags[16 * b : 16 * b + 16, 128 * r : 128 * r + 128] for r in range(8)], 0
                ).astype(BF).reshape(8, 16, 128)
                for b in range(blocks)
            ]
            place = slice(qq * 128, qq * 128 + 128)
            for h in range(heads):
                cols = slice(h * 128, h * 128 + 128)
                fb = jnp.broadcast_to(near_b[h : h + 1, place], (16, 128)).astype(BF)[None]
                fd = jnp.broadcast_to(near_d[h : h + 1, place], (16, 128)).astype(BF)[None]
                for b in range(blocks):
                    rs = slice(b * 128, b * 128 + 128)
                    fa = fa_ref[rs, cols].reshape(8, 16, 128)
                    fc = fc_ref[rs, cols].reshape(8, 16, 128)
                    w = jnp.maximum(fa * fb, fc * fd) * tiles[b]
                    w_ref[h, rs, place] = w.reshape(128, 128)
        for h in range(heads):
            cols = slice(h * 128, h * 128 + 128)
            acc_ref[:, cols] += dot(w_ref[h], value_ref[span, cols])

    above = rows_n - 1 - z
    both = jnp.minimum(z, above)
    longer = jnp.where(above > z, 1, 0)
    paired = 2 * both * chunks

    def arrival(k):
        first = k < paired
        late = k - paired
        hop = jnp.where(first, k // (2 * chunks), both + late // chunks) + 1
        ch = jnp.where(first, (k % (2 * chunks)) // 2, (late + paired) % chunks)
        side = jnp.where(first, k % 2, longer)
        return jnp.where(side == 0, z - hop, z + hop), ch, side

    def take(k):
        o, ch, side = arrival(k)
        feat_copy(slab_chunk(o, ch), o, ch, side).wait_recv()

        @pl.when(jnp.where(side == 0, z < rows_n - 1, z > 0))
        def _():
            feat_copy(slab_chunk(o, ch), o, ch, side).start()

    def turn(k, carry):
        @pl.when(k >= chunks)
        def _():
            j = k - chunks
            take(j)
            o, ch, _ = arrival(j)
            rows = pl.ds(pl.multiple_of(o * shard + ch * chunk, chunk), chunk)
            project(slab_ref[rows, :], rows)

        o, ch, _ = arrival(jnp.maximum(k - chunks, 0))
        mine = k < chunks
        step(jnp.where(mine, z * chunks + k, o * chunks + ch))
        return carry

    lax.fori_loop(0, rows_n * chunks, turn, 0)

    scores = score_ref[0:heads, :]
    spread_of = jnp.max(scores, axis=1, keepdims=True) - jnp.min(scores, axis=1, keepdims=True)
    wide = jnp.where(jnp.max(spread_of, axis=0, keepdims=True) <= SPAN, 0.0, 1.0)
    back = order_matrix(128, True)
    for b in range(blocks):
        rs = slice(b * 128, b * 128 + 128)
        nums = []
        aux = jnp.where(lane == 40, wide, jnp.zeros((128, 128), F32))
        for h in range(heads):
            cols = slice(h * 128, h * 128 + 128)
            acc = acc_ref[rs, cols]
            nums.append(acc)
            first, second, _ = (p.astype(F32) for p in split3(acc))
            base = 0 if h % 2 else half
            aux = jnp.where(lane == base + h, first, aux)
            aux = jnp.where(lane == base + 8 + h, second, aux)
            for k, part in enumerate(split3(m_ref[rs, cols])):
                aux = jnp.where(lane == 16 + 4 * k + h, part.astype(F32), aux)
        pairs = [jnp.where(lane < half, nums[2 * k], nums[2 * k + 1]) for k in range(heads // 2)]
        send = jnp.concatenate(pairs + [aux], 1).astype(BF)
        send_ref[rs, :] = dot(back, send).astype(BF)

    def part_copy(k, to, who):
        return pltpu.make_async_remote_copy(
            src_ref=send_ref.at[pl.ds(pl.multiple_of(to * own, own), own), :],
            dst_ref=recv_ref.at[pl.ds(pl.multiple_of(who * own, own), own), :],
            send_sem=part_send.at[k],
            recv_sem=part_recv.at[k],
            device_id=(z, (c + k) % cols_n),
            device_id_type=mesh_id,
        )

    def send_part(k, carry):
        part_copy(k, (c + k) % cols_n, c).start()
        return carry

    lax.fori_loop(1, cols_n, send_part, 0)
    mine = pl.ds(pl.multiple_of(c * own, own), own)
    recv_ref[mine, :] = send_ref[mine, :]

    def end_part(k, carry):
        part_copy(k, (c + k) % cols_n, (c + cols_n - k) % cols_n).wait_recv()
        return carry

    lax.fori_loop(1, cols_n, end_part, 0)
    final_kernel(heads, cols_n, recv_ref, own_dst_ref, weight_ref, gsrc_ref, gdst_ref, out_ref)
    seen = jnp.max(recv_ref[:, units : units + 128].astype(F32), axis=0, keepdims=True)
    flag_ref[...] = jnp.broadcast_to(
        jnp.max(jnp.where(lane == 40, seen, 0.0), axis=1, keepdims=True), flag_ref.shape
    )

    def end_send(k, carry):
        part_copy(k, (c + k) % cols_n, c).wait_send()
        dst_copy(k, c).wait_send()
        return carry

    lax.fori_loop(1, cols_n, end_send, 0)

    def end_own(ch, carry):
        src = feats_ref.at[pl.ds(pl.multiple_of(ch * chunk, chunk), chunk), :]

        @pl.when(z < rows_n - 1)
        def _():
            feat_copy(src, z, ch, 0).wait_send()

        @pl.when(z > 0)
        def _():
            feat_copy(src, z, ch, 1).wait_send()

        return carry

    lax.fori_loop(0, chunks, end_own, 0)

    def end_relay(k, carry):
        o, ch, side = arrival(k)

        @pl.when(jnp.where(side == 0, z < rows_n - 1, z > 0))
        def _():
            feat_copy(slab_chunk(o, ch), o, ch, side).wait_send()

        return carry

    lax.fori_loop(0, (rows_n - 1) * chunks, end_relay, 0)


def body(
    src_feats, dst_feats, proj_weight, attn_src, attn_dst, tile_dst, tile_src, tile_live, tile_mask
):
    heads, half = attn_src.shape
    units = heads * half
    peers = lax.axis_size("col")
    own = dst_feats.shape[0]
    nd = own * peers
    blocks = nd // 128
    rows_n = lax.axis_size("row")
    shard = src_feats.shape[0]
    sources = shard * rows_n
    nsb = sources // 128
    slots = tile_mask.shape[1]
    pitch = slots + 8
    slot = jnp.arange(slots, dtype=jnp.int32)
    pair = jnp.where(slot < tile_live[0, 0], tile_dst[0] * nsb + tile_src[0], -1)
    hit = pair[None, :] == jnp.arange(blocks * nsb, dtype=jnp.int32)[:, None]
    inv = jnp.min(jnp.where(hit, slot[None, :], slots), axis=1)
    flat_src = attn_src.reshape(units)
    flat_dst = attn_dst.reshape(units)
    unit_head = jnp.arange(units) // half
    arows = jnp.where(jnp.arange(8)[:, None] == unit_head[None, :], flat_src[None, :], 0.0)
    acols = jnp.where(
        unit_head[:, None] == jnp.arange(heads * 128)[None, :] // 128, flat_dst[:, None], 0.0
    )
    same = unit_head[:, None] == unit_head[None, :]
    gsrc = jnp.where(same, flat_src[:, None], 0.0)
    gdst = jnp.where(same, flat_dst[:, None], 0.0)
    wide = jnp.arange(1024)
    expand = (
        jnp.arange(128)[:, None] == ((wide // 128) * 16 + (wide % 128) // 8)[None, :]
    ).astype(BF)
    vm = pl.BlockSpec(memory_space=pltpu.VMEM)
    chunks = shard // (GROUP * 128)
    fast, flag = pl.pallas_call(
        functools.partial(fused_kernel, heads, rows_n, peers),
        out_shape=(
            jax.ShapeDtypeStruct((own, units), BF),
            jax.ShapeDtypeStruct((8, 128), F32),
        ),
        in_specs=[pl.BlockSpec(memory_space=pltpu.SMEM)] + [vm] * 8 + [pl.BlockSpec(memory_space=pl.ANY)],
        out_specs=(vm, vm),
        scratch_shapes=[
            pltpu.VMEM((16 * pitch, 128), jnp.int32),
            pltpu.VMEM((sources, src_feats.shape[1]), BF),
            pltpu.VMEM((nd, src_feats.shape[1]), BF),
            pltpu.VMEM((sources, heads * 128), BF),
            pltpu.VMEM((8, sources), F32),
            pltpu.VMEM((nd, heads * 128), BF),
            pltpu.VMEM((nd, heads * 128), BF),
            pltpu.VMEM((nd, heads * 128), F32),
            pltpu.VMEM((heads, nd, GROUP * 128), BF),
            pltpu.VMEM((nd, heads * 128), F32),
            pltpu.VMEM((nd, units + 128), BF),
            pltpu.VMEM((nd, units + 128), BF),
            pltpu.SemaphoreType.DMA((16,)),
            pltpu.SemaphoreType.DMA((2, rows_n * chunks)),
            pltpu.SemaphoreType.DMA((rows_n * chunks,)),
            pltpu.SemaphoreType.DMA((peers,)),
            pltpu.SemaphoreType.DMA((peers,)),
            pltpu.SemaphoreType.DMA((peers,)),
            pltpu.SemaphoreType.DMA((peers,)),
        ],
        compiler_params=pltpu.CompilerParams(
            vmem_limit_bytes=56 * 1024 * 1024, collective_id=0, has_side_effects=True
        ),
    )(inv, src_feats, dst_feats, proj_weight, arows, acols, expand, gsrc, gdst, tile_mask[0])

    def gathered(part, axis, count):
        copies = jnp.broadcast_to(part[None], (count,) + part.shape)
        return lax.all_to_all(copies, axis, 0, 0).reshape(count * part.shape[0], part.shape[1])

    def general(_):
        slab = gathered(src_feats, "row", rows_n)
        dst_all = gathered(dst_feats, "col", peers)
        send = pl.pallas_call(
            functools.partial(main_kernel, heads),
            out_shape=jax.ShapeDtypeStruct((nd, units + 128), BF),
            in_specs=[pl.BlockSpec(memory_space=pltpu.SMEM)]
            + [vm] * 6
            + [pl.BlockSpec(memory_space=pl.ANY)],
            out_specs=vm,
            scratch_shapes=[
                pltpu.VMEM((16 * pitch, 128), jnp.int32),
                pltpu.VMEM((sources, heads * 128), BF),
                pltpu.VMEM((8, sources), F32),
                pltpu.VMEM((nd, heads * 128), F32),
                pltpu.VMEM((nd, heads * 128), F32),
                pltpu.VMEM((nd, heads * 128), F32),
                pltpu.SemaphoreType.DMA((16,)),
            ],
            compiler_params=pltpu.CompilerParams(vmem_limit_bytes=56 * 1024 * 1024),
        )(inv, slab, dst_all, proj_weight, arows, acols, expand, tile_mask[0])
        recv = lax.all_to_all(send, "col", split_axis=0, concat_axis=0, tiled=True)
        return pl.pallas_call(
            functools.partial(final_kernel, heads, peers),
            out_shape=jax.ShapeDtypeStruct((own, units), BF),
            in_specs=[vm] * 5,
            out_specs=vm,
        )(recv, dst_feats, proj_weight, gsrc, gdst)

    return lax.cond(flag[0, 0] > 0, general, lambda kept: kept, fast)


def solution(mesh):
    placed = (
        P(("row", "col"), None),
        P(("row", "col"), None),
        P(),
        P(),
        P(),
        P("row", "col"),
        P("row", "col"),
        P("row", "col"),
        P("row", "col", None),
    )
    return jax.shard_map(
        body, mesh=mesh, in_specs=placed, out_specs=P(("row", "col"), None), check_vma=False
    )
```
